256 devices in a mesh: cuts: 4 (over y), blk: 64 (over x, z, core).
Axes of the slice: x: 4, y: 4, z: 8, core: 2. Of those that a mesh axis runs over, the one named last changes fastest.
Arguments:
- gap_load: float32 [4, 128, 2, 256, 128], P('cuts', 'blk'), may hold values from -24 to 24
- offsets: int32 [4, 128, 2], P('cuts', 'blk'), may hold values from -1 to 255, as said below
- corner_map: int32 [4, 128, 4], P('cuts', 'blk'), may hold values from -1 to 511, as said below
- flexibility: float32 [4, 128, 1024, 1024], P('cuts', 'blk'), may hold values from -0.5 to 4.5, as said below
- coupling: float32 [4, 128, 12, 1024], P('cuts', 'blk'), may hold values from -1.25 to 1.25
- corner_rows: float32 [4, 128, 12, 1536], P('cuts', 'blk'), may hold values from -0.1 to 1.1, as said below
Outputs:
- multipliers: float32 [4, 128, 2, 256, 128], P('cuts', 'blk')
- residual: float32 [4, 128, 2, 256, 128], P('cuts', 'blk')
The draws below stay inside these ranges and needn't reach their ends.
Inputs may be any that keep to these rules, and one draw needn't show every extreme that they name: `offsets`: on an interface owned by a subdomain, the neighbour's dof k matches the owner's dof (k + offset) mod 256; -1 marks an interface without multipliers: the tunnel's far end, or one that touches an excavated subdomain. `corner_map`: entries k = 0, 1, 2, 3 are the corners at near-left, near-right, far-left, far-right. Entry 2 of subdomain (r, c) is never -1, and every node is entry 2 of exactly one subdomain; the same node is entry 3 of (r, (c - 1) mod 128) and, for r + 1 < 4, entries 0 of (r + 1, c) and 1 of (r + 1, (c - 1) mod 128), and no other entry. -1 marks a clamped corner at the tunnel's near end. `flexibility`: each block is symmetric positive definite. `corner_rows`: row 3 k + j of a subdomain is row 3 m + j of one symmetric positive definite matrix of order 3 * 512, with m = corner_map entry k; zero rows where that entry is -1.
All inputs are finite; a program needn't handle non-finite values.
Results may differ from the reference program's by a relative error of at most 0.00021.
Values sent between devices are 32-bit elements; how exact they have to be, the bound alone decides.
A program may use at most 64 MiB of HBM per device.

```python
import math
import jax
import jax.numpy as jnp
from jax import lax

FD = 256
NI = 1024
NRHS = 128
ITERS = 3
CYCLES = 4
NCIRC = 128
NCORN = 512


def corner_numbers(key):
    ordering = jax.random.permutation(jax.random.fold_in(key, 11), NCORN).astype(jnp.int32)
    nodes = jnp.concatenate([jnp.full((1, NCIRC), -1, jnp.int32), ordering.reshape(CYCLES, NCIRC)], axis=0)
    nearer = nodes[:-1]
    farther = nodes[1:]
    return jnp.stack([nearer, jnp.roll(nearer, -1, axis=1), farther, jnp.roll(farther, -1, axis=1)], axis=-1).astype(jnp.int32)


def symmetric_part(key, order_size):
    spread = 0.45 / math.sqrt(order_size)
    uniform_draw = jax.random.uniform(key, (order_size, order_size), jnp.float32, -spread, spread)
    return (uniform_draw + uniform_draw.T) * 0.7071067811865476


def draw_corner_map(key, part):
    return corner_numbers(key)


def draw_corner_rows(key, part):
    numbers = corner_numbers(key)
    dof_count = 3 * NCORN
    matrix = jnp.eye(dof_count, dtype=jnp.float32) + symmetric_part(jax.random.fold_in(key, 12), dof_count)
    spread = 3 * jnp.maximum(numbers, 0)[..., None] + jnp.arange(3, dtype=jnp.int32)
    spread = spread.reshape(CYCLES, NCIRC, 12)
    picked = matrix[spread]
    keep = jnp.repeat(numbers >= 0, 3, axis=-1)[..., None]
    return jnp.where(keep, picked, 0.0).astype(jnp.float32)


def draw_flexibility(key, part):

    def one_block(sub_key):
        base = jnp.eye(NI, dtype=jnp.float32) + symmetric_part(jax.random.fold_in(sub_key, 1), NI)
        scales = jnp.exp(jax.random.uniform(jax.random.fold_in(sub_key, 2), (NI,), jnp.float32, math.log(0.7), math.log(1.4)))
        return scales[:, None] * base * scales[None, :]
    sub_keys = jax.random.split(key, CYCLES * NCIRC)
    return lax.map(one_block, sub_keys).reshape(CYCLES, NCIRC, NI, NI)


def draw_offsets(key, part):
    cycle_index = jnp.arange(CYCLES)[:, None]
    excavated = (jax.random.randint(jax.random.fold_in(key, 21), (CYCLES, NCIRC), 0, 8) == 0) & (cycle_index > 0)
    excavated_next = jnp.concatenate([excavated[1:], jnp.ones((1, NCIRC), jnp.bool_)], axis=0)
    far_open = ~excavated & ~excavated_next
    right_open = ~excavated & ~jnp.roll(excavated, -1, axis=1)
    values = jax.random.permutation(jax.random.fold_in(key, 22), 2 * CYCLES * NCIRC) % FD
    values = values.astype(jnp.int32).reshape(CYCLES, NCIRC, 2)
    values = values.at[0, 0, 1].set(FD - 1)
    return jnp.where(jnp.stack([far_open, right_open], axis=-1), values, -1).astype(jnp.int32)


def draw_gap_load(key, part):
    shape = (CYCLES, NCIRC, 2, FD, NRHS)
    cycle_pos = jnp.arange(CYCLES, dtype=jnp.float32) / CYCLES
    circ_pos = jnp.arange(NCIRC, dtype=jnp.float32) / NCIRC
    factor = 1.0 + cycle_pos[:, None] + circ_pos[None, :]
    base = jnp.clip(jax.random.normal(key, shape, jnp.float32), -6.0, 6.0)
    return base * factor[:, :, None, None, None]


def steps_of(own_key, extent, cuts, low, largest):
    def one(axis_at, blocks):
        draws = jax.random.uniform(jax.random.fold_in(jax.random.fold_in(own_key, 6), axis_at), (blocks,), jnp.float32, low / len(cuts), largest / len(cuts))
        return jnp.repeat(jnp.exp(draws), extent[axis_at] // blocks).reshape((-1,) + (1,) * (len(extent) - axis_at - 1))

    gain = one(*cuts[0])
    for cut in cuts[1:]:
        gain = gain * one(*cut)
    return gain


def noise(stream_key, extent, deviation, limit, cuts=(), kind=jnp.bfloat16):
    array = deviation * jax.random.normal(stream_key, extent, jnp.float32)
    if cuts:
        array = array * steps_of(stream_key, extent, cuts, -0.22, 0.18)
    return jnp.clip(array, -limit, limit).astype(kind)


def setup_inputs(seed: int = 0) -> dict:
    streams_of = jax.random.split(jax.random.key(seed), 7)
    gap_load = draw_gap_load(jax.random.fold_in(streams_of[6], 71), 0)
    offsets = draw_offsets(jax.random.fold_in(streams_of[6], 71), 0)
    corner_map = draw_corner_map(jax.random.fold_in(streams_of[6], 71), 0)
    flexibility = draw_flexibility(jax.random.fold_in(streams_of[6], 71), 0)
    coupling = noise(streams_of[4], (CYCLES, NCIRC, 12, NI), 0.08, 1.25, ((0, 4), (1, 64)), jnp.float32)
    corner_rows = draw_corner_rows(jax.random.fold_in(streams_of[6], 71), 0)
    return dict(gap_load=gap_load, offsets=offsets, corner_map=corner_map, flexibility=flexibility, coupling=coupling, corner_rows=corner_rows)


HIGH = lax.Precision.HIGHEST


def rotate(values, amounts, orient):
    face_size = values.shape[-2]
    indices = (jnp.arange(face_size, dtype=jnp.int32) + orient * amounts[..., None]) % face_size
    return jnp.take_along_axis(values, indices[..., None].astype(jnp.int32), axis=-2)


def corner_indices(corner_map, dof_count):
    spread = 3 * corner_map[..., None] + jnp.arange(3, dtype=jnp.int32)
    spread = jnp.where(corner_map[..., None] >= 0, spread, dof_count)
    return spread.reshape(corner_map.shape[0], corner_map.shape[1], 12).astype(jnp.int32)


def operator(direction, offsets, flexibility, coupling, corner_rows, corner_dofs):
    cycle_count, circ_count, _, face_size, load_count = direction.shape
    sent_far = -rotate(direction[:, :, 0], offsets[:, :, 0], 1)
    sent_right = -rotate(direction[:, :, 1], offsets[:, :, 1], 1)
    nearside = jnp.concatenate([jnp.zeros_like(sent_far[:1]), sent_far[:-1]], axis=0)
    leftside = jnp.roll(sent_right, 1, axis=1)
    loads = jnp.stack([nearside, direction[:, :, 0], leftside, direction[:, :, 1]], axis=2)
    loads = loads.reshape(cycle_count, circ_count, 4 * face_size, load_count)
    corner_terms = jnp.einsum("rcki,rcin->rckn", coupling, loads, precision=HIGH)
    coarse = jnp.zeros((corner_rows.shape[-1], load_count), jnp.float32)
    coarse = coarse.at[corner_dofs.reshape(-1)].add(corner_terms.reshape(-1, load_count), mode="drop")
    corner_values = jnp.einsum("rckm,mn->rckn", corner_rows, coarse, precision=HIGH)
    moved = jnp.einsum("rcij,rcjn->rcin", flexibility, loads, precision=HIGH)
    moved = moved + jnp.einsum("rcki,rckn->rcin", coupling, corner_values, precision=HIGH)
    moved = moved.reshape(cycle_count, circ_count, 4, face_size, load_count)
    far_near = jnp.concatenate([moved[1:, :, 0], jnp.zeros_like(moved[:1, :, 0])], axis=0)
    right_left = jnp.roll(moved[:, :, 2], -1, axis=1)
    jump_far = moved[:, :, 1] - rotate(far_near, offsets[:, :, 0], -1)
    jump_right = moved[:, :, 3] - rotate(right_left, offsets[:, :, 1], -1)
    active = (offsets >= 0).astype(jnp.float32)[..., None, None]
    return jnp.stack([jump_far, jump_right], axis=2) * active


def inner_sum(first, second):
    return jnp.sum(first * second, axis=(0, 1, 2, 3))


def reference(gap_load, offsets, corner_map, flexibility, coupling, corner_rows):
    active = (offsets >= 0).astype(jnp.float32)[..., None, None]
    corner_dofs = corner_indices(corner_map, corner_rows.shape[-1])
    residual = gap_load * active
    direction = residual
    multipliers = jnp.zeros_like(residual)
    norm_now = inner_sum(residual, residual)
    for iteration in range(ITERS):
        mapped = operator(direction, offsets, flexibility, coupling, corner_rows, corner_dofs)
        step_size = norm_now / inner_sum(direction, mapped)
        multipliers = multipliers + step_size * direction
        residual = residual - step_size * mapped
        norm_next = inner_sum(residual, residual)
        direction = residual + (norm_next / norm_now) * direction
        norm_now = norm_next
    return multipliers, residual
```

```python
import functools

import jax
import jax.numpy as jnp
from jax import lax
from jax.experimental import pallas as pl
from jax.experimental.pallas import tpu as pltpu
from jax.sharding import PartitionSpec as P

MESH = pl.DeviceIdType.MESH
F32, BF16 = jnp.float32, jnp.bfloat16
FD, RHS = 256, 128
NEAR, FAR, LEFT, RIGHT = 0, 1, 2, 3
BLOCK = 40
APPS = 3


def halves(value):
    high = value.astype(BF16)
    return high, (value - high.astype(F32)).astype(BF16)


def quadrants(product):
    rows = product.shape[0] // 2
    wide = product[:rows] + product[rows:]
    return wide[:, :RHS] + wide[:, RHS:]


def face(index):
    return slice(index * FD, (index + 1) * FD)


def scratch(ny, nx, nz, dofs):
    dma = pltpu.SemaphoreType.DMA
    rounds = APPS + 1
    return dict(
        stage=pltpu.VMEM((4, FD, 4 * FD), F32),
        flex_parts=pltpu.VMEM((2, 2, 4 * FD, 4 * FD), BF16),
        info=pltpu.VMEM((8, 128), jnp.int32),
        info_near=pltpu.VMEM((8, 128), jnp.int32),
        info_left=pltpu.VMEM((8, 128), jnp.int32),
        word_near=pltpu.SMEM((8, 128), jnp.int32),
        word_left=pltpu.SMEM((8, 128), jnp.int32),
        coup_pad=pltpu.VMEM((128, 4 * FD), F32),
        coup_t=pltpu.VMEM((2, 4 * FD, 128), BF16),
        coup_t_n=pltpu.VMEM((6, FD, 128), BF16),
        coup_far=pltpu.VMEM((2, 12, FD), F32),
        coup_near=pltpu.VMEM((2, 12, FD), F32),
        coup_left=pltpu.VMEM((12, FD), F32),
        coup_right=pltpu.VMEM((12, FD), F32),
        node_pad=pltpu.VMEM((32, 4 * FD), F32),
        node_rows=pltpu.VMEM((2, 64, 4 * FD), BF16),
        rows_mate=pltpu.VMEM((2, 12, dofs), F32),
        rows_pad=pltpu.VMEM((64, dofs), F32),
        rows_parts=pltpu.VMEM((128, dofs), BF16),
        pick=pltpu.VMEM((nz * BLOCK, dofs), BF16),
        coarse=pltpu.VMEM((nx, 128, nz * BLOCK), BF16),
        line=pltpu.VMEM((rounds, ny, 32, RHS), F32),
        blocks=pltpu.VMEM((rounds, nx, nz, BLOCK, RHS), F32),
        gap_near=pltpu.VMEM((2, FD, RHS), F32),
        gap_left=pltpu.VMEM((FD, RHS), F32),
        vec=pltpu.VMEM((5, 2, 4 * FD, RHS), F32),
        split=pltpu.VMEM((2, 4 * FD, 2 * RHS), BF16),
        moved=pltpu.VMEM((APPS, 2, 4 * FD, RHS), F32),
        total=pltpu.VMEM((2, 4 * FD, RHS), F32),
        face_far=pltpu.VMEM((APPS, 2, FD, RHS), F32),
        face_near=pltpu.VMEM((APPS, 2, FD, RHS), F32),
        face_left=pltpu.VMEM((APPS, FD, RHS), F32),
        face_right=pltpu.VMEM((APPS, FD, RHS), F32),
        twice=pltpu.VMEM((8, 2 * FD, RHS), F32),
        mate_out=pltpu.VMEM((APPS, 40, RHS), F32),
        mate_in=pltpu.VMEM((APPS, 40, RHS), F32),
        y_own=pltpu.VMEM((APPS, 2, 16, RHS), F32),
        y_far=pltpu.VMEM((APPS, 2, 16, RHS), F32),
        y_near=pltpu.VMEM((APPS, 2, 16, RHS), F32),
        y_left=pltpu.VMEM((APPS, 16, RHS), F32),
        y_right=pltpu.VMEM((APPS, 16, RHS), F32),
        own=pltpu.VMEM((6, 2, 2, FD, RHS), F32),
        end_y=pltpu.VMEM((ny, 8, RHS), F32),
        end_z=pltpu.VMEM((nz, 8, RHS), F32),
        end_x=pltpu.VMEM((nx, 8, RHS), F32),
        end_out=pltpu.VMEM((8, RHS), F32),
        end_in=pltpu.VMEM((8, RHS), F32),
        stage_sem=dma((4,)),
        word_sem=dma((2,)),
        setup_sem=dma((2, 10)),
        y_sem=dma((2, rounds, ny - 1)),
        z_sem=dma((2, rounds, nz - 1)),
        x_sem=dma((2, rounds, nx - 1, nz)),
        face_sem=dma((2, APPS, 4)),
        mate_sem=dma((2, APPS)),
        yv_sem=dma((2, APPS, 4)),
        end_sem=dma((2, ny + nx + nz - 2)),
    )


def kernel(ny, nx, nz, names, gap, offs, cmap, coup, rows, flex, mult_out, res_out, *refs):
    s = dict(zip(names, refs))
    y, b = lax.axis_index("cuts"), lax.axis_index("blk")
    nb = 2 * nx * nz
    k = lax.rem(b, 2)
    z = lax.rem(b // 2, nz)
    x = b // (2 * nz)
    at = lambda xx, zz, kk: (xx * nz + zz) * 2 + kk
    up, down = lax.rem(y + 1, ny), lax.rem(y + ny - 1, ny)
    right, left = lax.rem(b + 1, nb), lax.rem(b + nb - 1, nb)
    mate = at(x, z, 1 - k)
    y_peers = [(lax.rem(y + d, ny), b) for d in range(1, ny)]
    z_peers = [(y, at(x, lax.rem(z + d, nz), k)) for d in range(1, nz)]
    x_peers = [(y, at(lax.rem(x + d, nx), z, k)) for d in range(1, nx)]
    started = []

    def send(src, dst, sems, index, peer):
        copy = pltpu.make_async_remote_copy(
            src_ref=src,
            dst_ref=dst,
            send_sem=sems.at[(0,) + index],
            recv_sem=sems.at[(1,) + index],
            device_id=peer,
            device_id_type=MESH,
        )
        copy.start()
        started.append(copy)
        return copy

    def fetch(chunk):
        sub, part = divmod(chunk, 4)
        return pltpu.make_async_copy(
            flex.at[0, sub, face(part), :], s["stage"].at[chunk % 4], s["stage_sem"].at[chunk % 4]
        )

    for chunk in range(4):
        fetch(chunk).start()

    greeted = y_peers + z_peers + x_peers + [(y, right), (y, left)]
    barrier = pltpu.get_barrier_semaphore()
    for peer in greeted:
        pl.semaphore_signal(barrier, inc=1, device_id=peer, device_id_type=MESH)

    row = lax.broadcasted_iota(jnp.int32, (16, RHS), 0)
    slot = jnp.where(row < 3, 0, jnp.where(row < 6, 1, 2))
    node = jnp.where(row < 3, cmap[0, 0, 2], jnp.where(row < 6, cmap[0, 1, 2], cmap[0, 1, 3]))
    number = jnp.where(row < 9, 3 * node + row - 3 * slot, -1).astype(F32)
    s["line"][0, y] = jnp.concatenate([number, jnp.full((16, RHS), -1.0, F32)], axis=0)
    row8 = lax.broadcasted_iota(jnp.int32, (8, 128), 0)
    s["info"][...] = jnp.where(row8 == 0, offs[0, 0, 0], jnp.where(row8 == 1, offs[0, 1, 0], offs[0, 1, 1]))

    pl.semaphore_wait(barrier, len(greeted))

    def line_sends(rd):
        return [
            send(s["line"].at[rd, y], s["line"].at[rd, y], s["y_sem"], (rd, d), peer)
            for d, peer in enumerate(y_peers)
        ]

    def block_sends(rd):
        own = s["blocks"].at[rd, x, z]
        zs = [send(own, own, s["z_sem"], (rd, d), peer) for d, peer in enumerate(z_peers)]
        xs = [send(own, own, s["x_sem"], (rd, d, 0), peer) for d, peer in enumerate(x_peers)]
        return zs, xs

    order = sorted(range(1, nz), key=lambda d: min(d, nz - d))

    def forward(rd, zs):
        xs = []
        for d in order:
            zs[d - 1].wait_recv()
            got = s["blocks"].at[rd, x, lax.rem(z + nz - d, nz)]
            xs += [send(got, got, s["x_sem"], (rd, e, d), peer) for e, peer in enumerate(x_peers)]
        return xs

    number_line = line_sends(0)
    setup = s["setup_sem"]
    got_gap_near = send(gap.at[0, :, 0], s["gap_near"], setup, (0,), (up, b))
    got_gap_left = send(gap.at[0, 1, 1], s["gap_left"], setup, (1,), (y, right))
    got_info_near = send(s["info"], s["info_near"], setup, (2,), (up, b))
    got_info_left = send(s["info"], s["info_left"], setup, (3,), (y, right))
    got_rows = send(rows.at[0], s["rows_mate"], setup, (4,), (y, mate))
    got_coup = [
        send(coup.at[0, :, :, face(NEAR)], s["coup_far"], setup, (5,), (down, b)),
        send(coup.at[0, :, :, face(FAR)], s["coup_near"], setup, (6,), (up, b)),
        send(coup.at[0, 1, :, face(RIGHT)], s["coup_left"], setup, (7,), (y, right)),
        send(coup.at[0, 0, :, face(LEFT)], s["coup_right"], setup, (8,), (y, left)),
    ]

    not_first = jnp.where(y > 0, 1.0, 0.0).astype(F32)
    not_last = jnp.where(y < ny - 1, 1.0, 0.0).astype(F32)
    for sub in range(2):
        s["node_pad"][...] = jnp.zeros((32, 4 * FD), F32)
        s["node_pad"][3 * sub : 3 * sub + 6] = coup[0, sub, 6:12]
        s["node_pad"][16 + 3 * sub : 22 + 3 * sub] = coup[0, sub, 0:6] * not_first
        high, low = halves(s["node_pad"][...])
        s["node_rows"][sub, 0:32] = high
        s["node_rows"][sub, 32:64] = low

    def transposed(value):
        width = value.shape[1]
        pad = s["coup_pad"]
        high = value.astype(BF16).astype(F32)
        low = value - high
        pad[:, 0:width] = jnp.zeros((128, width), F32)
        pad[0:12, 0:width] = high
        pad[16:28, 0:width] = low
        pad[32:44, 0:width] = high
        pad[48:60, 0:width] = low
        return pad[:, 0:width].T.astype(BF16)

    for sub in range(2):
        s["coup_t"][sub] = transposed(coup[0, sub])

    def make_block(rd):
        own = s["blocks"].at[rd, x, z]
        for cycle in range(ny):
            value = s["line"][rd, cycle, 0:9]
            if rd > 0 and cycle + 1 < ny:
                value = value + s["line"][rd, cycle + 1, 16:25]
            own[9 * cycle : 9 * cycle + 9] = value
        if rd > 0:
            sums = s["line"][rd, 0, 9:13]
            for cycle in range(1, ny):
                sums = sums + s["line"][rd, cycle, 9:13]
        else:
            sums = jnp.full((4, RHS), -1.0, F32)
        own[9 * ny : 9 * ny + 4] = sums
        if 9 * ny + 4 < BLOCK:
            own[9 * ny + 4 : BLOCK] = jnp.full((BLOCK - 9 * ny - 4, RHS), -1.0, F32)

    for copy in number_line:
        copy.wait_recv()
    make_block(0)
    number_z, number_x = block_sends(0)

    def rolled(index, value, start):
        s["twice"][index, 0:FD] = value
        s["twice"][index, FD : 2 * FD] = value
        return s["twice"][index, pl.ds(start, FD)]

    ahead = lambda off: lax.rem(off + FD, FD)
    back = lambda off: lax.rem(FD - off, FD)
    on = lambda off: jnp.where(off >= 0, 1.0, 0.0).astype(F32)
    got_info_near.wait_recv()
    got_info_left.wait_recv()
    words = [
        pltpu.make_async_copy(s["info_near"], s["word_near"], s["word_sem"].at[0]),
        pltpu.make_async_copy(s["info_left"], s["word_left"], s["word_sem"].at[1]),
    ]
    for copy in words:
        copy.start()
    for copy in words:
        copy.wait()
    off_far = [offs[0, sub, 0] for sub in range(2)]
    off_right = [offs[0, sub, 1] for sub in range(2)]
    off_near = [s["word_near"][sub, 0] for sub in range(2)]
    off_left = s["word_left"][2, 0]
    on_far = [on(off) for off in off_far]
    on_right = [on(off) for off in off_right]
    on_near = [on(off) * not_first for off in off_near]
    on_left = on(off_left)

    for chunk in range(8):
        sub, part = divmod(chunk, 4)
        fetch(chunk).wait()

        @pl.loop(0, FD // 32)
        def _(step):
            at_row = pl.multiple_of(step * 32, 32)
            high, low = halves(s["stage"][chunk % 4, pl.ds(at_row, 32)])
            base = FD * (part % 2)
            s["flex_parts"][sub, part // 2, pl.ds(base + at_row, 32)] = high
            s["flex_parts"][sub, part // 2, pl.ds(2 * FD + base + at_row, 32)] = low

        if chunk + 4 < 8:
            fetch(chunk + 4).start()

    got_gap_near.wait_recv()
    got_gap_left.wait_recv()
    r0, w0, q0, w1, q1 = (s["vec"].at[i] for i in range(5))
    for sub in range(2):
        r0[sub, face(FAR)] = gap[0, sub, 0] * on_far[sub]
        r0[sub, face(RIGHT)] = gap[0, sub, 1] * on_right[sub]
        r0[sub, face(NEAR)] = rolled(sub, s["gap_near"][sub], ahead(off_near[sub])) * -on_near[sub]
    r0[0, face(LEFT)] = rolled(2, s["gap_left"][...], ahead(off_left)) * -on_left
    r0[1, face(LEFT)] = rolled(3, gap[0, 0, 1], ahead(off_right[0])) * -on_right[0]

    owned = [(sub, part) for sub in range(2) for part in range(2)]

    def dot(first, second):
        total = None
        for sub, part in owned:
            term = jnp.sum(first(sub, part) * second(sub, part), axis=0, keepdims=True)
            total = term if total is None else total + term
        return total

    def of(vector):
        return lambda sub, part: vector[sub, face(2 * part + 1)]

    def product(sub, group):
        wide = jnp.dot(s["flex_parts"][sub, group], s["split"][sub], preferred_element_type=F32)
        s["moved"][app, sub, 2 * FD * group : 2 * FD * (group + 1)] = quadrants(wide)

    def stacked(value):
        high, low = halves(value)
        return jnp.concatenate([high, high, low, low, jnp.zeros((64, RHS), BF16)], axis=0)

    def begin(vector, dots):
        rd = app + 1
        for sub in range(2):
            high, low = halves(vector[sub])
            s["split"][sub, :, 0:RHS] = high
            s["split"][sub, :, RHS : 2 * RHS] = low
        wide = jnp.dot(s["node_rows"][0], s["split"][0], preferred_element_type=F32)
        wide = wide + jnp.dot(s["node_rows"][1], s["split"][1], preferred_element_type=F32)
        tile = s["line"].at[rd, y]
        tile[...] = quadrants(wide)
        tile[9:11] = jnp.concatenate(dots, axis=0)
        return line_sends(rd)

    def finish_faces(result, last):
        moved = s["total"]
        for sub in range(2):
            term = jnp.dot(s["coup_t"][sub], stacked(s["y_own"][app, sub]), preferred_element_type=F32)
            moved[sub] = s["moved"][app, sub] + term

        def other(index, value, y_value):
            return value + jnp.dot(s["coup_t_n"][index], stacked(y_value), preferred_element_type=F32)

        inner_left, inner_right = moved[1, face(LEFT)], moved[0, face(RIGHT)]
        result[0, face(RIGHT)] = (inner_right - rolled(0, inner_left, back(off_right[0]))) * on_right[0]
        if not last:
            result[1, face(LEFT)] = (inner_left - rolled(1, inner_right, ahead(off_right[0]))) * on_right[0]
        for copy in got_y:
            copy.wait_recv()
        for copy in got_faces:
            copy.wait_recv()
        for sub in range(2):
            value = other(sub, s["face_far"][app, sub], s["y_far"][app, sub]) * not_last
            jump = moved[sub, face(FAR)] - rolled(2 + sub, value, back(off_far[sub]))
            result[sub, face(FAR)] = jump * on_far[sub]
            if not last:
                value = other(2 + sub, s["face_near"][app, sub], s["y_near"][app, sub])
                jump = moved[sub, face(NEAR)] - rolled(4 + sub, value, ahead(off_near[sub]))
                result[sub, face(NEAR)] = jump * on_near[sub]
        value = other(5, s["face_right"][app], s["y_right"][app])
        jump = moved[1, face(RIGHT)] - rolled(6, value, back(off_right[1]))
        result[1, face(RIGHT)] = jump * on_right[1]
        if not last:
            value = other(4, s["face_left"][app], s["y_left"][app])
            jump = moved[0, face(LEFT)] - rolled(7, value, ahead(off_left))
            result[0, face(LEFT)] = jump * on_left

    def update(target, base, factor, step):
        for sub in range(2):
            for part in range(4):
                target[sub, face(part)] = base[sub, face(part)] + factor * step[sub, face(part)]

    none = jnp.zeros((1, RHS), F32)
    r1, p1, x2, r2, s1, w2 = (s["own"].at[i] for i in range(6))
    plain = lambda vector: lambda sub, part: vector[sub, part]
    gamma, delta = [], []
    for app in range(APPS):
        last = app == APPS - 1
        if app == 0:
            vector, result, dots = r0, w0, [dot(of(r0), of(r0)), none]
        elif app == 1:
            vector, result, dots = w0, q0, [none, dot(of(r0), of(w0))]
        else:
            vector, result = w1, q1
            dots = [dot(plain(r1), plain(r1)), dot(plain(r1), of(w1))]
        got_line = begin(vector, dots)
        moved = s["moved"].at[app]
        for sub in range(2):
            product(sub, 0)
        got_faces = [send(moved.at[:, face(NEAR)], s["face_far"].at[app], s["face_sem"], (app, 0), (down, b))]
        if not last:
            got_faces.append(
                send(moved.at[:, face(FAR)], s["face_near"].at[app], s["face_sem"], (app, 1), (up, b))
            )
        if app == 0:
            number_x += forward(0, number_z)
        for copy in got_line:
            copy.wait_recv()
        make_block(app + 1)
        got_z, got_x = block_sends(app + 1)
        for sub in range(2):
            product(sub, 1)
        got_faces.append(
            send(moved.at[0, face(LEFT)], s["face_right"].at[app], s["face_sem"], (app, 2), (y, left))
        )
        if not last:
            got_faces.append(
                send(moved.at[1, face(RIGHT)], s["face_left"].at[app], s["face_sem"], (app, 3), (y, right))
            )
        if app == 0:
            got_rows.wait_recv()
            s["rows_pad"][...] = jnp.zeros(s["rows_pad"].shape, F32)
            for sub in range(2):
                s["rows_pad"][16 * sub : 16 * sub + 12] = rows[0, sub]
                s["rows_pad"][32 + 16 * sub : 44 + 16 * sub] = s["rows_mate"][sub]
            high, low = halves(s["rows_pad"][...])
            s["rows_parts"][0:64] = high
            s["rows_parts"][64:128] = low
            for copy in number_x:
                copy.wait_recv()
            dofs = s["pick"].shape[1]
            for xx in range(nx):
                numbers = s["blocks"][0, xx].reshape(nz * BLOCK, RHS)
                for q in range(dofs // 128):
                    lane = (lax.broadcasted_iota(jnp.int32, numbers.shape, 1) + 128 * q).astype(F32)
                    s["pick"][:, 128 * q : 128 * q + 128] = jnp.where(numbers == lane, 1.0, 0.0).astype(BF16)
                picked = lax.dot_general(
                    s["rows_parts"][...],
                    s["pick"][...],
                    (((1,), (1,)), ((), ())),
                    preferred_element_type=F32,
                )
                s["coarse"][xx] = picked.astype(BF16)
            for copy in got_coup:
                copy.wait_recv()
            for sub in range(2):
                s["coup_t_n"][sub] = transposed(s["coup_far"][sub])
                s["coup_t_n"][2 + sub] = transposed(s["coup_near"][sub])
            s["coup_t_n"][4] = transposed(s["coup_left"][...])
            s["coup_t_n"][5] = transposed(s["coup_right"][...])
        got_x += forward(app + 1, got_z)
        for copy in got_x:
            copy.wait_recv()
        wide = None
        sums = None
        for xx in range(nx):
            loads = s["blocks"][app + 1, xx]
            part = jnp.sum(loads[:, BLOCK - 8 :, :], axis=0)
            sums = part if sums is None else sums + part
            high, low = halves(loads.reshape(nz * BLOCK, RHS))
            term = jnp.dot(
                s["coarse"][xx], jnp.concatenate([high, low], axis=1), preferred_element_type=F32
            )
            wide = term if wide is None else wide + term
        ysum = quadrants(wide)
        s["mate_out"][app, 0:32] = ysum[32:64]
        s["mate_out"][app, 32:40] = sums
        mate_copy = send(s["mate_out"].at[app], s["mate_in"].at[app], s["mate_sem"], (app,), (y, mate))
        mate_copy.wait_recv()
        sums = sums + s["mate_in"][app, 32:40]
        for sub in range(2):
            s["y_own"][app, sub] = ysum[16 * sub : 16 * sub + 16] + s["mate_in"][app, 16 * sub : 16 * sub + 16]
        y_own = s["y_own"].at[app]
        got_y = [
            send(y_own, s["y_far"].at[app], s["yv_sem"], (app, 0), (down, b)),
            send(y_own.at[0], s["y_right"].at[app], s["yv_sem"], (app, 2), (y, left)),
        ]
        if not last:
            got_y += [
                send(y_own, s["y_near"].at[app], s["yv_sem"], (app, 1), (up, b)),
                send(y_own.at[1], s["y_left"].at[app], s["yv_sem"], (app, 3), (y, right)),
            ]
        finish_faces(result, last)
        first_row = 9 * ny - (BLOCK - 8)
        if app == 0:
            gamma.append(sums[first_row : first_row + 1])
        elif app == 1:
            delta.append(sums[first_row + 1 : first_row + 2])
            alpha0 = gamma[0] / delta[0]
            update(w1, w0, -alpha0, q0)
            for sub, part in owned:
                own = face(2 * part + 1)
                r1[sub, part] = r0[sub, own] - alpha0 * w0[sub, own]
        else:
            gamma.append(sums[first_row : first_row + 1])
            delta.append(sums[first_row + 1 : first_row + 2])

    beta1 = gamma[1] / gamma[0]
    alpha1 = gamma[1] / (delta[1] - beta1 * gamma[1] / alpha0)
    for sub, part in owned:
        own = face(2 * part + 1)
        z1 = q1[sub, own] + beta1 * q0[sub, own]
        s_value = w1[sub, own] + beta1 * w0[sub, own]
        p_value = r1[sub, part] + beta1 * r0[sub, own]
        s1[sub, part] = s_value
        p1[sub, part] = p_value
        x2[sub, part] = alpha0 * r0[sub, own] + alpha1 * p_value
        r2[sub, part] = r1[sub, part] - alpha1 * s_value
        w2[sub, part] = w1[sub, own] - alpha1 * z1

    sums = jnp.concatenate(
        [dot(plain(r2), plain(r2)), dot(plain(r2), plain(w2)), jnp.zeros((6, RHS), F32)], axis=0
    )
    base = 0
    for buffer, here, peers in (
        (s["end_y"], y, y_peers),
        (s["end_z"], z, z_peers),
        (s["end_x"], x, x_peers),
    ):
        buffer[here] = sums
        copies = [
            send(buffer.at[here], buffer.at[here], s["end_sem"], (base + d,), peer)
            for d, peer in enumerate(peers)
        ]
        base += len(peers)
        for copy in copies:
            copy.wait_recv()
        sums = jnp.sum(buffer[...], axis=0)
    s["end_out"][...] = sums
    send(s["end_out"], s["end_in"], s["end_sem"], (base,), (y, mate)).wait_recv()
    sums = sums + s["end_in"][...]
    gamma2, delta2 = sums[0:1], sums[1:2]
    beta2 = gamma2 / gamma[1]
    alpha2 = gamma2 / (delta2 - beta2 * gamma2 / alpha1)
    for sub, part in owned:
        mult_out[0, sub, part] = x2[sub, part] + alpha2 * (r2[sub, part] + beta2 * p1[sub, part])
        res_out[0, sub, part] = r2[sub, part] - alpha2 * (w2[sub, part] + beta2 * s1[sub, part])
    for copy in started:
        copy.wait_send()


def per_device(ny, nx, nz, gap_load, offsets, corner_map, flexibility, coupling, corner_rows):
    shapes = scratch(ny, nx, nz, corner_rows.shape[-1])
    vmem, smem = (pl.BlockSpec(memory_space=space) for space in (pltpu.VMEM, pltpu.SMEM))
    out = jax.ShapeDtypeStruct(gap_load.shape, F32)
    return pl.pallas_call(
        functools.partial(kernel, ny, nx, nz, tuple(shapes)),
        out_shape=(out, out),
        in_specs=[vmem, smem, smem, vmem, vmem, pl.BlockSpec(memory_space=pl.ANY)],
        out_specs=(vmem, vmem),
        scratch_shapes=list(shapes.values()),
        compiler_params=pltpu.CompilerParams(
            collective_id=0, has_side_effects=True, vmem_limit_bytes=60 * 1024 * 1024
        ),
    )(gap_load, offsets, corner_map, coupling, corner_rows, flexibility)


def solution(mesh):
    ny, nb = mesh.shape["cuts"], mesh.shape["blk"]
    nz = 8 if nb == 64 else 2
    nx = nb // (2 * nz)
    in_specs = (
        P("cuts", "blk", None, None, None),
        P("cuts", "blk", None),
        P("cuts", "blk", None),
        P("cuts", "blk", None, None),
        P("cuts", "blk", None, None),
        P("cuts", "blk", None, None),
    )
    out_specs = (P("cuts", "blk", None, None, None), P("cuts", "blk", None, None, None))
    return jax.shard_map(
        functools.partial(per_device, ny, nx, nz),
        mesh=mesh,
        in_specs=in_specs,
        out_specs=out_specs,
        check_vma=False,
    )
```

```python
import functools
import types

import jax
import jax.numpy as jnp
from jax import lax
from jax.experimental import pallas as pl
from jax.experimental.pallas import tpu as pltpu
from jax.sharding import PartitionSpec as P

MESH = pl.DeviceIdType.MESH
F32, BF16 = jnp.float32, jnp.bfloat16
FD, RHS = 256, 128
NEAR, FAR, LEFT, RIGHT = 0, 1, 2, 3
BLOCK = 40
APPS = 3


def halves(value):
    high = value.astype(BF16)
    return high, (value - high.astype(F32)).astype(BF16)


def quadrants(product):
    rows = product.shape[0] // 2
    wide = product[:rows] + product[rows:]
    return wide[:, :RHS] + wide[:, RHS:]


def face(index):
    return slice(index * FD, (index + 1) * FD)


def scratch(ny, nx, nz, dofs):
    dma = pltpu.SemaphoreType.DMA
    rounds = APPS + 1
    return dict(
        gap=pltpu.VMEM((1, 2, 2, FD, RHS), F32),
        coup=pltpu.VMEM((12, 2, 4 * FD), F32),
        rows=pltpu.VMEM((12, 2, dofs), F32),
        offs=pltpu.SMEM((1, 2, 2), jnp.int32),
        cmap=pltpu.SMEM((1, 2, 4), jnp.int32),
        stage=pltpu.VMEM((4, FD, 4 * FD), F32),
        flex_parts=pltpu.VMEM((2, 2, 4 * FD, 4 * FD), BF16),
        info=pltpu.VMEM((8, 128), jnp.int32),
        info_near=pltpu.VMEM((8, 128), jnp.int32),
        info_left=pltpu.VMEM((8, 128), jnp.int32),
        word_near=pltpu.SMEM((8, 128), jnp.int32),
        word_left=pltpu.SMEM((8, 128), jnp.int32),
        coup_pad=pltpu.VMEM((128, 4 * FD), F32),
        coup_t=pltpu.VMEM((2, 4 * FD, 128), BF16),
        coup_t_n=pltpu.VMEM((6, FD, 128), BF16),
        coup_far=pltpu.VMEM((12, 2, FD), F32),
        coup_near=pltpu.VMEM((12, 2, FD), F32),
        coup_left=pltpu.VMEM((12, 2, FD), F32),
        coup_right=pltpu.VMEM((12, 2, FD), F32),
        node_pad=pltpu.VMEM((32, 4 * FD), F32),
        node_rows=pltpu.VMEM((2, 64, 4 * FD), BF16),
        rows_pad=pltpu.VMEM((24, dofs), F32),
        rows_parts=pltpu.VMEM((64, dofs), BF16),
        pick=pltpu.VMEM((nz * BLOCK, dofs), BF16),
        picked=pltpu.VMEM((nx, 2, 24, nz * BLOCK), F32),
        picked_in=pltpu.VMEM((nx, 2, 24, nz * BLOCK), F32),
        coarse=pltpu.VMEM((2 * nx * 48, nz * BLOCK), BF16),
        number_y=pltpu.VMEM((ny, 8, 128), F32),
        number_z=pltpu.VMEM((nz, 8, 128), F32),
        number_x=pltpu.VMEM((nx, 2, 8, 128), F32),
        line=pltpu.VMEM((APPS, ny, 32, RHS), F32),
        blocks=pltpu.VMEM((APPS, nz, BLOCK, RHS), F32),
        gap_near=pltpu.VMEM((2, FD, RHS), F32),
        gap_left=pltpu.VMEM((FD, RHS), F32),
        vec=pltpu.VMEM((5, 2, 4 * FD, RHS), F32),
        split=pltpu.VMEM((2, 4 * FD, 2 * RHS), BF16),
        moved=pltpu.VMEM((APPS, 2, 4 * FD, RHS), F32),
        total=pltpu.VMEM((2, 4 * FD, RHS), F32),
        face_far=pltpu.VMEM((APPS, 2, FD, RHS), F32),
        face_near=pltpu.VMEM((APPS, 2, FD, RHS), F32),
        face_left=pltpu.VMEM((APPS, FD, RHS), F32),
        face_right=pltpu.VMEM((APPS, FD, RHS), F32),
        twice=pltpu.VMEM((8, 2 * FD, RHS), F32),
        part_out=pltpu.VMEM((APPS, nx, 2, 32, RHS), F32),
        part_in=pltpu.VMEM((APPS, nx, 2, 32, RHS), F32),
        y_own=pltpu.VMEM((APPS, 2, 16, RHS), F32),
        y_far=pltpu.VMEM((APPS, 2, 16, RHS), F32),
        y_near=pltpu.VMEM((APPS, 2, 16, RHS), F32),
        y_left=pltpu.VMEM((APPS, 16, RHS), F32),
        y_right=pltpu.VMEM((APPS, 16, RHS), F32),
        own=pltpu.VMEM((6, 2, 2, FD, RHS), F32),
        end_y=pltpu.VMEM((ny, 8, RHS), F32),
        end_z=pltpu.VMEM((nz, 8, RHS), F32),
        end_x=pltpu.VMEM((nx, 2, 8, RHS), F32),
        stage_sem=dma((4,)),
        load_sem=dma((5,)),
        word_sem=dma((2,)),
        setup_sem=dma((2, 10)),
        y_sem=dma((2, rounds, ny - 1)),
        z_sem=dma((2, rounds, nz - 1)),
        x_sem=dma((2, rounds, 2 * nx - 1)),
        pick_sem=dma((2, 2 * nx - 1)),
        face_sem=dma((2, APPS, 4)),
        yv_sem=dma((2, APPS, 4)),
        end_sem=dma((2, ny + 2 * nx + nz - 3)),
    )


def kernel(ny, nx, nz, names, gap_in, offs_in, cmap_in, coup_in, rows_in, flex, mult_out, res_out, *refs):
    s = types.SimpleNamespace(**dict(zip(names, refs)))
    y, b = lax.axis_index("cuts"), lax.axis_index("blk")
    nb = 2 * nx * nz
    k = lax.rem(b, 2)
    z = lax.rem(b // 2, nz)
    x = b // (2 * nz)
    at = lambda xx, zz, kk: (xx * nz + zz) * 2 + kk
    up, down = lax.rem(y + 1, ny), lax.rem(y + ny - 1, ny)
    right, left = lax.rem(b + 1, nb), lax.rem(b + nb - 1, nb)
    y_peers = [(lax.rem(y + d, ny), b) for d in range(1, ny)]
    z_peers = [(y, at(x, lax.rem(z + d, nz), k)) for d in range(1, nz)]
    x_line = [(lax.rem(x + d, nx), lax.rem(k + e, 2)) for d in range(nx) for e in range(2)]
    x_peers = [(y, at(xx, z, kk)) for xx, kk in x_line[1:]]
    started = []

    def send(src, dst, sems, index, peer):
        copy = pltpu.make_async_remote_copy(
            src_ref=src,
            dst_ref=dst,
            send_sem=sems.at[(0,) + index],
            recv_sem=sems.at[(1,) + index],
            device_id=peer,
            device_id_type=MESH,
        )
        copy.start()
        started.append(copy)
        return copy

    greeted = y_peers + z_peers + x_peers + [(y, right), (y, left)]
    barrier = pltpu.get_barrier_semaphore()
    for peer in greeted:
        pl.semaphore_signal(barrier, inc=1, device_id=peer, device_id_type=MESH)

    loads = [
        pltpu.make_async_copy(source, getattr(s, name), s.load_sem.at[i])
        for i, (name, source) in enumerate(
            dict(cmap=cmap_in, offs=offs_in, gap=gap_in, coup=coup_in, rows=rows_in).items()
        )
    ]
    for copy in loads:
        copy.start()
    chunks = [(sub, 2 * group + part) for group in range(2) for sub in range(2) for part in range(2)]

    def fetch(chunk):
        sub, part = chunks[chunk]
        return pltpu.make_async_copy(
            flex.at[0, sub, face(part), :], s.stage.at[chunk % 4], s.stage_sem.at[chunk % 4]
        )

    for chunk in range(4):
        fetch(chunk).start()

    loads[0].wait()
    loads[1].wait()
    gap, offs, cmap, coup, rows = s.gap, s.offs, s.cmap, s.coup, s.rows

    lane = lax.broadcasted_iota(jnp.int32, (8, 128), 1) - 9 * y
    slot = jnp.where(lane < 3, 0, jnp.where(lane < 6, 1, 2))
    node = jnp.where(lane < 3, cmap[0, 0, 2], jnp.where(lane < 6, cmap[0, 1, 2], cmap[0, 1, 3]))
    here = (lane >= 0) & (lane < 9) & (lax.broadcasted_iota(jnp.int32, (8, 128), 0) == z)
    s.number_y[y] = jnp.where(here, 3 * node + lane - 3 * slot, 0).astype(F32)
    row8 = lax.broadcasted_iota(jnp.int32, (8, 128), 0)
    s.info[...] = jnp.where(row8 == 0, offs[0, 0, 0], jnp.where(row8 == 1, offs[0, 1, 0], offs[0, 1, 1]))

    pl.semaphore_wait(barrier, len(greeted))

    def to_all(buffer, sems, rd, peers):
        return [send(buffer, buffer, sems, (rd, d), peer) for d, peer in enumerate(peers)]

    number_copies = to_all(s.number_y.at[y], s.y_sem, 0, y_peers)
    setup = s.setup_sem
    got_gap_near = send(gap_in.at[0, :, 0], s.gap_near, setup, (0,), (up, b))
    got_gap_left = send(gap_in.at[0, 1, 1], s.gap_left, setup, (1,), (y, right))
    got_info_near = send(s.info, s.info_near, setup, (2,), (up, b))
    got_info_left = send(s.info, s.info_left, setup, (3,), (y, right))
    got_coup = [
        send(coup_in.at[:, :, face(NEAR)], s.coup_far, setup, (5,), (down, b)),
        send(coup_in.at[:, :, face(FAR)], s.coup_near, setup, (6,), (up, b)),
        send(coup_in.at[:, :, face(RIGHT)], s.coup_left, setup, (7,), (y, right)),
        send(coup_in.at[:, :, face(LEFT)], s.coup_right, setup, (8,), (y, left)),
    ]

    def unpack(target, first, matrix, sub):
        for i in range(12):
            target[first + i : first + i + 1, 0 : matrix.shape[2]] = matrix[i, sub : sub + 1]

    for copy in loads[2:]:
        copy.wait()
    not_first = jnp.where(y > 0, 1.0, 0.0).astype(F32)
    not_last = jnp.where(y < ny - 1, 1.0, 0.0).astype(F32)
    for sub in range(2):
        unpack(s.coup_pad, 0, coup, sub)
        s.node_pad[...] = jnp.zeros((32, 4 * FD), F32)
        s.node_pad[3 * sub : 3 * sub + 6] = s.coup_pad[6:12]
        s.node_pad[16 + 3 * sub : 22 + 3 * sub] = s.coup_pad[0:6] * not_first
        high, low = halves(s.node_pad[...])
        s.node_rows[sub, 0:32] = high
        s.node_rows[sub, 32:64] = low

    def transposed(matrix, sub):
        width = matrix.shape[2]
        pad = s.coup_pad
        unpack(pad, 0, matrix, sub)
        value = pad[0:12, 0:width]
        high = value.astype(BF16).astype(F32)
        low = value - high
        pad[:, 0:width] = jnp.zeros((128, width), F32)
        pad[0:12, 0:width] = high
        pad[16:28, 0:width] = low
        pad[32:44, 0:width] = high
        pad[48:60, 0:width] = low
        return pad[:, 0:width].T.astype(BF16)

    for sub in range(2):
        s.coup_t[sub] = transposed(coup, sub)

    def make_block():
        own = s.blocks.at[app, z]
        for cycle in range(ny):
            value = s.line[app, cycle, 0:9]
            if cycle + 1 < ny:
                value = value + s.line[app, cycle + 1, 16:25]
            own[9 * cycle : 9 * cycle + 9] = value
        sums = s.line[app, 0, 9:13]
        for cycle in range(1, ny):
            sums = sums + s.line[app, cycle, 9:13]
        own[9 * ny : 9 * ny + 4] = sums

    for copy in number_copies:
        copy.wait_recv()
    s.number_z[z] = jnp.sum(s.number_y[...], axis=0)
    number_copies = to_all(s.number_z.at[z], s.z_sem, 0, z_peers)

    def rolled(index, value, start):
        s.twice[index, 0:FD] = value
        s.twice[index, FD : 2 * FD] = value
        return s.twice[index, pl.ds(start, FD)]

    ahead = lambda off: lax.rem(off + FD, FD)
    back = lambda off: lax.rem(FD - off, FD)
    on = lambda off: jnp.where(off >= 0, 1.0, 0.0).astype(F32)
    got_info_near.wait_recv()
    got_info_left.wait_recv()
    words = [
        pltpu.make_async_copy(s.info_near, s.word_near, s.word_sem.at[0]),
        pltpu.make_async_copy(s.info_left, s.word_left, s.word_sem.at[1]),
    ]
    for copy in words:
        copy.start()
    for copy in words:
        copy.wait()
    off_far = [offs[0, sub, 0] for sub in range(2)]
    off_right = [offs[0, sub, 1] for sub in range(2)]
    off_near = [s.word_near[sub, 0] for sub in range(2)]
    off_left = s.word_left[2, 0]
    on_far = [on(off) for off in off_far]
    on_right = [on(off) for off in off_right]
    on_near = [on(off) * not_first for off in off_near]
    on_left = on(off_left)

    def convert(turn):
        sub, part = chunks[turn]
        fetch(turn).wait()

        @pl.loop(0, FD // 64)
        def _(step):
            at_row = pl.multiple_of(step * 64, 64)
            high, low = halves(s.stage[turn % 4, pl.ds(at_row, 64)])
            base = FD * (part % 2)
            s.flex_parts[sub, part // 2, pl.ds(base + at_row, 64)] = high
            s.flex_parts[sub, part // 2, pl.ds(2 * FD + base + at_row, 64)] = low

        if turn + 4 < 8:
            fetch(turn + 4).start()

    for turn in range(4):
        convert(turn)

    for copy in number_copies:
        copy.wait_recv()
    s.number_x[x, k] = jnp.sum(s.number_z[...], axis=0)
    number_copies = to_all(s.number_x.at[x, k], s.x_sem, 0, x_peers)

    for sub in range(2):
        unpack(s.rows_pad, 12 * sub, rows, sub)
    high, low = halves(jnp.concatenate([s.rows_pad[...], jnp.zeros((8, rows.shape[2]), F32)], axis=0))
    s.rows_parts[0:32] = high
    s.rows_parts[32:64] = low
    s.y_own[...] = jnp.zeros(s.y_own.shape, F32)

    got_gap_near.wait_recv()
    got_gap_left.wait_recv()
    r0, w0, q0, w1, q1 = (s.vec.at[i] for i in range(5))
    for sub in range(2):
        r0[sub, face(FAR)] = gap[0, sub, 0] * on_far[sub]
        r0[sub, face(RIGHT)] = gap[0, sub, 1] * on_right[sub]
        r0[sub, face(NEAR)] = rolled(sub, s.gap_near[sub], ahead(off_near[sub])) * -on_near[sub]
    r0[0, face(LEFT)] = rolled(2, s.gap_left[...], ahead(off_left)) * -on_left
    r0[1, face(LEFT)] = rolled(3, gap[0, 0, 1], ahead(off_right[0])) * -on_right[0]

    owned = [(sub, part) for sub in range(2) for part in range(2)]

    def dot(first, second):
        total = None
        for sub, part in owned:
            term = jnp.sum(first(sub, part) * second(sub, part), axis=0, keepdims=True)
            total = term if total is None else total + term
        return total

    def of(vector):
        return lambda sub, part: vector[sub, face(2 * part + 1)]

    def product(sub, group):
        wide = jnp.dot(s.flex_parts[sub, group], s.split[sub], preferred_element_type=F32)
        s.moved[app, sub, 2 * FD * group : 2 * FD * (group + 1)] = quadrants(wide)

    def stacked(value):
        high, low = halves(value)
        return jnp.concatenate([high, high, low, low, jnp.zeros((64, RHS), BF16)], axis=0)

    def begin(vector, dots):
        for sub in range(2):
            high, low = halves(vector[sub])
            s.split[sub, :, 0:RHS] = high
            s.split[sub, :, RHS : 2 * RHS] = low
        wide = jnp.dot(s.node_rows[0], s.split[0], preferred_element_type=F32)
        wide = wide + jnp.dot(s.node_rows[1], s.split[1], preferred_element_type=F32)
        tile = s.line.at[app, y]
        tile[...] = quadrants(wide)
        tile[9:11] = jnp.concatenate(dots, axis=0)
        return to_all(tile, s.y_sem, app + 1, y_peers)

    def finish_faces(result, last):
        moved = s.total
        for sub in range(2):
            term = jnp.dot(s.coup_t[sub], stacked(s.y_own[app, sub]), preferred_element_type=F32)
            moved[sub] = s.moved[app, sub] + term

        def other(index, value, y_value):
            return value + jnp.dot(s.coup_t_n[index], stacked(y_value), preferred_element_type=F32)

        inner_left, inner_right = moved[1, face(LEFT)], moved[0, face(RIGHT)]
        result[0, face(RIGHT)] = (inner_right - rolled(0, inner_left, back(off_right[0]))) * on_right[0]
        if not last:
            result[1, face(LEFT)] = (inner_left - rolled(1, inner_right, ahead(off_right[0]))) * on_right[0]
        for copy in got_y:
            copy.wait_recv()
        for copy in got_faces:
            copy.wait_recv()
        for sub in range(2):
            value = other(sub, s.face_far[app, sub], s.y_far[app, sub]) * not_last
            jump = moved[sub, face(FAR)] - rolled(2 + sub, value, back(off_far[sub]))
            result[sub, face(FAR)] = jump * on_far[sub]
            if not last:
                value = other(2 + sub, s.face_near[app, sub], s.y_near[app, sub])
                jump = moved[sub, face(NEAR)] - rolled(4 + sub, value, ahead(off_near[sub]))
                result[sub, face(NEAR)] = jump * on_near[sub]
        value = other(5, s.face_right[app], s.y_right[app])
        jump = moved[1, face(RIGHT)] - rolled(6, value, back(off_right[1]))
        result[1, face(RIGHT)] = jump * on_right[1]
        if not last:
            value = other(4, s.face_left[app], s.y_left[app])
            jump = moved[0, face(LEFT)] - rolled(7, value, ahead(off_left))
            result[0, face(LEFT)] = jump * on_left

    def update(target, base, factor, step):
        for sub in range(2):
            for part in range(4):
                target[sub, face(part)] = base[sub, face(part)] + factor * step[sub, face(part)]

    none = jnp.zeros((1, RHS), F32)
    r1, p1, x2, r2, s1, w2 = (s.own.at[i] for i in range(6))
    plain = lambda vector: lambda sub, part: vector[sub, part]
    gamma, delta = [], []
    for app in range(APPS):
        last = app == APPS - 1
        if app == 0:
            vector, result, dots = r0, w0, [dot(of(r0), of(r0)), none]
        elif app == 1:
            vector, result, dots = w0, q0, [none, dot(of(r0), of(w0))]
        else:
            vector, result = w1, q1
            dots = [dot(plain(r1), plain(r1)), dot(plain(r1), of(w1))]
        got_line = begin(vector, dots)
        moved = s.moved.at[app]
        for sub in range(2):
            product(sub, 0)
        got_faces = [send(moved.at[:, face(NEAR)], s.face_far.at[app], s.face_sem, (app, 0), (down, b))]
        if not last:
            got_faces.append(
                send(moved.at[:, face(FAR)], s.face_near.at[app], s.face_sem, (app, 1), (up, b))
            )
        for copy in got_line:
            copy.wait_recv()
        make_block()
        got_z = to_all(s.blocks.at[app, z], s.z_sem, app + 1, z_peers)
        if app == 0:
            for turn in range(4, 8):
                convert(turn)
        for sub in range(2):
            product(sub, 1)
        got_faces.append(
            send(moved.at[0, face(LEFT)], s.face_right.at[app], s.face_sem, (app, 2), (y, left))
        )
        if not last:
            got_faces.append(
                send(moved.at[1, face(RIGHT)], s.face_left.at[app], s.face_sem, (app, 3), (y, right))
            )
        if app == 0:
            for copy in number_copies:
                copy.wait_recv()
            dofs = s.pick.shape[1]
            lane = lax.broadcasted_iota(jnp.int32, (8, 128), 1)
            got_picked = []
            for i, (xx, kk) in enumerate(x_line):
                tile = jnp.where(lane < 9 * ny, s.number_x[xx, kk], -1.0)
                column = jnp.concatenate([tile, jnp.zeros((120, 128), F32)], axis=0).T
                numbers = jnp.concatenate(
                    [jnp.broadcast_to(column[0:BLOCK, j : j + 1], (BLOCK, 128)) for j in range(nz)], axis=0
                )
                for q in range(dofs // 128):
                    wanted = (lax.broadcasted_iota(jnp.int32, numbers.shape, 1) + 128 * q).astype(F32)
                    s.pick[:, 128 * q : 128 * q + 128] = jnp.where(numbers == wanted, 1.0, 0.0).astype(BF16)
                both = lax.dot_general(
                    s.rows_parts[...],
                    s.pick[...],
                    (((1,), (1,)), ((), ())),
                    preferred_element_type=F32,
                )
                own_rows = both[0:24] + both[32:56]
                if i == 0:
                    s.picked_in[x, k] = own_rows
                else:
                    s.picked[xx, kk] = own_rows
                    got_picked.append(
                        send(s.picked.at[xx, kk], s.picked_in.at[x, k], s.pick_sem, (i - 1,), x_peers[i - 1])
                    )
            for copy in got_coup:
                copy.wait_recv()
            for sub in range(2):
                s.coup_t_n[sub] = transposed(s.coup_far, sub)
                s.coup_t_n[2 + sub] = transposed(s.coup_near, sub)
            s.coup_t_n[4] = transposed(s.coup_left, 1)
            s.coup_t_n[5] = transposed(s.coup_right, 0)
            for copy in got_picked:
                copy.wait_recv()
            for i in range(2 * nx):
                high, low = halves(s.picked_in[i // 2, i % 2])
                s.coarse[24 * i : 24 * i + 24] = high
                s.coarse[48 * nx + 24 * i : 48 * nx + 24 * i + 24] = low
        for copy in got_z:
            copy.wait_recv()
        loads = s.blocks[app]
        sums = jnp.sum(loads[:, BLOCK - 8 :, :], axis=0)
        high, low = halves(loads.reshape(nz * BLOCK, RHS))
        wide = jnp.dot(s.coarse[...], jnp.concatenate([high, low], axis=1), preferred_element_type=F32)
        parts = quadrants(wide)
        for i in range(2 * nx):
            s.part_out[app, i // 2, i % 2, 0:24] = parts[24 * i : 24 * i + 24]
            s.part_out[app, i // 2, i % 2, 24:32] = sums
        got_parts = []
        for i, (xx, kk) in enumerate(x_line):
            if i == 0:
                s.part_in[app, x, k] = s.part_out[app, x, k]
            else:
                got_parts.append(
                    send(
                        s.part_out.at[app, xx, kk],
                        s.part_in.at[app, x, k],
                        s.x_sem,
                        (app + 1, i - 1),
                        x_peers[i - 1],
                    )
                )
        for copy in got_parts:
            copy.wait_recv()
        ysum = s.part_in[app, 0, 0]
        for i in range(1, 2 * nx):
            ysum = ysum + s.part_in[app, i // 2, i % 2]
        sums = ysum[24:32]
        for sub in range(2):
            s.y_own[app, sub, 0:12] = ysum[12 * sub : 12 * sub + 12]
        y_own = s.y_own.at[app]
        got_y = [
            send(y_own, s.y_far.at[app], s.yv_sem, (app, 0), (down, b)),
            send(y_own.at[0], s.y_right.at[app], s.yv_sem, (app, 2), (y, left)),
        ]
        if not last:
            got_y += [
                send(y_own, s.y_near.at[app], s.yv_sem, (app, 1), (up, b)),
                send(y_own.at[1], s.y_left.at[app], s.yv_sem, (app, 3), (y, right)),
            ]
        finish_faces(result, last)
        first_row = 9 * ny - (BLOCK - 8)
        if app == 0:
            gamma.append(sums[first_row : first_row + 1])
        elif app == 1:
            delta.append(sums[first_row + 1 : first_row + 2])
            alpha0 = gamma[0] / delta[0]
            update(w1, w0, -alpha0, q0)
            for sub, part in owned:
                own = face(2 * part + 1)
                r1[sub, part] = r0[sub, own] - alpha0 * w0[sub, own]
        else:
            gamma.append(sums[first_row : first_row + 1])
            delta.append(sums[first_row + 1 : first_row + 2])

    beta1 = gamma[1] / gamma[0]
    alpha1 = gamma[1] / (delta[1] - beta1 * gamma[1] / alpha0)
    for sub, part in owned:
        own = face(2 * part + 1)
        z1 = q1[sub, own] + beta1 * q0[sub, own]
        s_value = w1[sub, own] + beta1 * w0[sub, own]
        p_value = r1[sub, part] + beta1 * r0[sub, own]
        s1[sub, part] = s_value
        p1[sub, part] = p_value
        x2[sub, part] = alpha0 * r0[sub, own] + alpha1 * p_value
        r2[sub, part] = r1[sub, part] - alpha1 * s_value
        w2[sub, part] = w1[sub, own] - alpha1 * z1

    sums = jnp.concatenate(
        [dot(plain(r2), plain(r2)), dot(plain(r2), plain(w2)), jnp.zeros((6, RHS), F32)], axis=0
    )
    base = 0
    for buffer, here, peers in (
        (s.end_y, (y,), y_peers),
        (s.end_z, (z,), z_peers),
        (s.end_x, (x, k), x_peers),
    ):
        buffer[here] = sums
        copies = [
            send(buffer.at[here], buffer.at[here], s.end_sem, (base + d,), peer)
            for d, peer in enumerate(peers)
        ]
        base += len(peers)
        for copy in copies:
            copy.wait_recv()
        sums = jnp.sum(buffer[...], axis=tuple(range(len(here))))
    gamma2, delta2 = sums[0:1], sums[1:2]
    beta2 = gamma2 / gamma[1]
    alpha2 = gamma2 / (delta2 - beta2 * gamma2 / alpha1)
    for sub, part in owned:
        mult_out[0, sub, part] = x2[sub, part] + alpha2 * (r2[sub, part] + beta2 * p1[sub, part])
        res_out[0, sub, part] = r2[sub, part] - alpha2 * (w2[sub, part] + beta2 * s1[sub, part])
    for copy in started:
        copy.wait_send()


def hand_on(mult_in, res_in, mult_out, res_out):
    mult_out[...] = mult_in[...]
    res_out[...] = res_in[...]


def per_device(ny, nx, nz, gap_load, offsets, corner_map, flexibility, coupling, corner_rows):
    shapes = scratch(ny, nx, nz, corner_rows.shape[-1])
    vmem, hbm = (pl.BlockSpec(memory_space=space) for space in (pltpu.VMEM, pltpu.HBM))
    out = jax.ShapeDtypeStruct(gap_load.shape, F32)

    results = pl.pallas_call(
        functools.partial(kernel, ny, nx, nz, tuple(shapes)),
        out_shape=(out, out),
        in_specs=[hbm] * 6,
        out_specs=(vmem, vmem),
        scratch_shapes=list(shapes.values()),
        compiler_params=pltpu.CompilerParams(
            collective_id=0, has_side_effects=True, vmem_limit_bytes=60 * 1024 * 1024
        ),
    )(gap_load, offsets, corner_map, coupling[0].transpose(1, 0, 2), corner_rows[0].transpose(1, 0, 2), flexibility)
    return pl.pallas_call(
        hand_on, out_shape=(out, out), in_specs=[vmem, vmem], out_specs=(vmem, vmem)
    )(*results)


def solution(mesh):
    ny, nb = mesh.shape["cuts"], mesh.shape["blk"]
    nz = 8 if nb == 64 else 2
    nx = nb // (2 * nz)
    in_specs = (
        P("cuts", "blk", None, None, None),
        P("cuts", "blk", None),
        P("cuts", "blk", None),
        P("cuts", "blk", None, None),
        P("cuts", "blk", None, None),
        P("cuts", "blk", None, None),
    )
    out_specs = (P("cuts", "blk", None, None, None), P("cuts", "blk", None, None, None))
    return jax.shard_map(
        functools.partial(per_device, ny, nx, nz),
        mesh=mesh,
        in_specs=in_specs,
        out_specs=out_specs,
        check_vma=False,
    )
```

```python
import functools
import types

import jax
import jax.numpy as jnp
from jax import lax
from jax.experimental import pallas as pl
from jax.experimental.pallas import tpu as pltpu
from jax.sharding import PartitionSpec as P

MESH = pl.DeviceIdType.MESH
F32, BF16 = jnp.float32, jnp.bfloat16
FD, RHS = 256, 128
NEAR, FAR, LEFT, RIGHT = 0, 1, 2, 3
BLOCK = 40
APPS = 3


def halves(value):
    high = value.astype(BF16)
    return high, (value - high.astype(F32)).astype(BF16)


def quadrants(product):
    rows = product.shape[0] // 2
    wide = product[:rows] + product[rows:]
    return wide[:, :RHS] + wide[:, RHS:]


def face(index):
    return slice(index * FD, (index + 1) * FD)


def scratch(ny, nx, nz, dofs):
    dma = pltpu.SemaphoreType.DMA
    rounds = APPS + 1
    return dict(
        gap=pltpu.VMEM((1, 2, 2, FD, RHS), F32),
        coup=pltpu.VMEM((12, 2, 4 * FD), F32),
        rows=pltpu.VMEM((12, 2, dofs), F32),
        offs=pltpu.SMEM((1, 2, 2), jnp.int32),
        cmap=pltpu.SMEM((1, 2, 4), jnp.int32),
        stage=pltpu.VMEM((8, FD, 4 * FD), F32),
        flex_parts=pltpu.VMEM((2, 2, 4 * FD, 4 * FD), BF16),
        info=pltpu.VMEM((8, 128), jnp.int32),
        info_near=pltpu.VMEM((8, 128), jnp.int32),
        info_left=pltpu.VMEM((8, 128), jnp.int32),
        word_near=pltpu.SMEM((8, 128), jnp.int32),
        word_left=pltpu.SMEM((8, 128), jnp.int32),
        coup_pad=pltpu.VMEM((128, 4 * FD), F32),
        coup_t=pltpu.VMEM((2, 4 * FD, 128), BF16),
        coup_t_n=pltpu.VMEM((6, FD, 128), BF16),
        coup_far=pltpu.VMEM((12, 2, FD), F32),
        coup_near=pltpu.VMEM((12, 2, FD), F32),
        coup_left=pltpu.VMEM((12, 2, FD), F32),
        coup_right=pltpu.VMEM((12, 2, FD), F32),
        node_pad=pltpu.VMEM((32, 4 * FD), F32),
        node_rows=pltpu.VMEM((2, 64, 4 * FD), BF16),
        rows_pad=pltpu.VMEM((24, dofs), F32),
        rows_parts=pltpu.VMEM((64, dofs), BF16),
        pick=pltpu.VMEM((nz * BLOCK, dofs), BF16),
        picked=pltpu.VMEM((nx, 2, 24, nz * BLOCK), F32),
        picked_in=pltpu.VMEM((nx, 2, 24, nz * BLOCK), F32),
        coarse=pltpu.VMEM((2 * nx * 48, nz * BLOCK), BF16),
        number_y=pltpu.VMEM((ny, 8, 128), F32),
        number_z=pltpu.VMEM((nz, 8, 128), F32),
        number_x=pltpu.VMEM((nx, 2, 8, 128), F32),
        line=pltpu.VMEM((APPS, ny, 32, RHS), F32),
        blocks=pltpu.VMEM((APPS, nz, BLOCK, RHS), F32),
        gap_near=pltpu.VMEM((2, FD, RHS), F32),
        gap_left=pltpu.VMEM((FD, RHS), F32),
        vec=pltpu.VMEM((5, 2, 4 * FD, RHS), F32),
        split=pltpu.VMEM((2, 4 * FD, 2 * RHS), BF16),
        moved=pltpu.VMEM((APPS, 2, 4 * FD, RHS), F32),
        total=pltpu.VMEM((2, 4 * FD, RHS), F32),
        face_far=pltpu.VMEM((APPS, 2, FD, RHS), F32),
        face_near=pltpu.VMEM((APPS, 2, FD, RHS), F32),
        face_left=pltpu.VMEM((APPS, FD, RHS), F32),
        face_right=pltpu.VMEM((APPS, FD, RHS), F32),
        twice=pltpu.VMEM((8, 2 * FD, RHS), F32),
        part_out=pltpu.VMEM((APPS, nx, 2, 32, RHS), F32),
        part_in=pltpu.VMEM((APPS, nx, 2, 32, RHS), F32),
        y_own=pltpu.VMEM((APPS, 2, 16, RHS), F32),
        y_far=pltpu.VMEM((APPS, 2, 16, RHS), F32),
        y_near=pltpu.VMEM((APPS, 2, 16, RHS), F32),
        y_left=pltpu.VMEM((APPS, 16, RHS), F32),
        y_right=pltpu.VMEM((APPS, 16, RHS), F32),
        own=pltpu.VMEM((6, 2, 2, FD, RHS), F32),
        end_y=pltpu.VMEM((ny, 8, RHS), F32),
        end_z=pltpu.VMEM((nz, 8, RHS), F32),
        end_x=pltpu.VMEM((nx, 2, 8, RHS), F32),
        stage_sem=dma((8,)),
        load_sem=dma((5,)),
        word_sem=dma((2,)),
        setup_sem=dma((2, 10)),
        y_sem=dma((2, rounds, ny - 1)),
        z_sem=dma((2, rounds, nz - 1)),
        x_sem=dma((2, rounds, 2 * nx - 1)),
        pick_sem=dma((2, 2 * nx - 1)),
        face_sem=dma((2, APPS, 4)),
        yv_sem=dma((2, APPS, 4)),
        end_sem=dma((2, ny + 2 * nx + nz - 3)),
    )


def kernel(ny, nx, nz, names, gap_in, offs_in, cmap_in, coup_in, rows_in, flex, mult_out, res_out, *refs):
    s = types.SimpleNamespace(**dict(zip(names, refs)))
    y, b = lax.axis_index("cuts"), lax.axis_index("blk")
    nb = 2 * nx * nz
    k = lax.rem(b, 2)
    z = lax.rem(b // 2, nz)
    x = b // (2 * nz)
    at = lambda xx, zz, kk: (xx * nz + zz) * 2 + kk
    up, down = lax.rem(y + 1, ny), lax.rem(y + ny - 1, ny)
    right, left = lax.rem(b + 1, nb), lax.rem(b + nb - 1, nb)
    far_first = lambda n: sorted(range(1, n), key=lambda d: -min(d, n - d))
    y_peers = [(lax.rem(y + d, ny), b) for d in far_first(ny)]
    z_peers = [(y, at(x, lax.rem(z + d, nz), k)) for d in far_first(nz)]
    x_line = [(lax.rem(x + d, nx), lax.rem(k + e, 2)) for d in [0] + far_first(nx) for e in range(2)]
    x_peers = [(y, at(xx, z, kk)) for xx, kk in x_line[1:]]
    started = []

    def send(src, dst, sems, index, peer):
        copy = pltpu.make_async_remote_copy(
            src_ref=src,
            dst_ref=dst,
            send_sem=sems.at[(0,) + index],
            recv_sem=sems.at[(1,) + index],
            device_id=peer,
            device_id_type=MESH,
        )
        copy.start()
        started.append(copy)
        return copy

    greeted = y_peers + z_peers + x_peers + [(y, right), (y, left)]
    barrier = pltpu.get_barrier_semaphore()
    for peer in greeted:
        pl.semaphore_signal(barrier, inc=1, device_id=peer, device_id_type=MESH)

    loads = [
        pltpu.make_async_copy(source, getattr(s, name), s.load_sem.at[i])
        for i, (name, source) in enumerate(
            dict(cmap=cmap_in, offs=offs_in, gap=gap_in, coup=coup_in, rows=rows_in).items()
        )
    ]
    for copy in loads:
        copy.start()
    chunks = [(sub, 2 * group + part) for group in range(2) for sub in range(2) for part in range(2)]

    def fetch(chunk):
        sub, part = chunks[chunk]
        return pltpu.make_async_copy(
            flex.at[0, sub, face(part), :], s.stage.at[chunk], s.stage_sem.at[chunk]
        )

    for chunk in range(8):
        fetch(chunk).start()

    loads[0].wait()
    loads[1].wait()
    gap, offs, cmap, coup, rows = s.gap, s.offs, s.cmap, s.coup, s.rows

    lane = lax.broadcasted_iota(jnp.int32, (8, 128), 1) - 9 * y
    slot = jnp.where(lane < 3, 0, jnp.where(lane < 6, 1, 2))
    node = jnp.where(lane < 3, cmap[0, 0, 2], jnp.where(lane < 6, cmap[0, 1, 2], cmap[0, 1, 3]))
    here = (lane >= 0) & (lane < 9) & (lax.broadcasted_iota(jnp.int32, (8, 128), 0) == z)
    s.number_y[y] = jnp.where(here, 3 * node + lane - 3 * slot, 0).astype(F32)
    row8 = lax.broadcasted_iota(jnp.int32, (8, 128), 0)
    s.info[...] = jnp.where(row8 == 0, offs[0, 0, 0], jnp.where(row8 == 1, offs[0, 1, 0], offs[0, 1, 1]))

    pl.semaphore_wait(barrier, len(greeted))

    def to_all(buffer, sems, rd, peers):
        return [send(buffer, buffer, sems, (rd, d), peer) for d, peer in enumerate(peers)]

    number_copies = to_all(s.number_y.at[y], s.y_sem, 0, y_peers)
    setup = s.setup_sem
    got_gap_near = send(gap_in.at[0, :, 0], s.gap_near, setup, (0,), (up, b))
    got_gap_left = send(gap_in.at[0, 1, 1], s.gap_left, setup, (1,), (y, right))
    got_info_near = send(s.info, s.info_near, setup, (2,), (up, b))
    got_info_left = send(s.info, s.info_left, setup, (3,), (y, right))
    got_coup = [
        send(coup_in.at[:, :, face(NEAR)], s.coup_far, setup, (5,), (down, b)),
        send(coup_in.at[:, :, face(FAR)], s.coup_near, setup, (6,), (up, b)),
        send(coup_in.at[:, :, face(RIGHT)], s.coup_left, setup, (7,), (y, right)),
        send(coup_in.at[:, :, face(LEFT)], s.coup_right, setup, (8,), (y, left)),
    ]

    def unpack(target, first, matrix, sub):
        for i in range(12):
            target[first + i : first + i + 1, 0 : matrix.shape[2]] = matrix[i, sub : sub + 1]

    for copy in loads[2:]:
        copy.wait()
    not_first = jnp.where(y > 0, 1.0, 0.0).astype(F32)
    not_last = jnp.where(y < ny - 1, 1.0, 0.0).astype(F32)
    for sub in range(2):
        unpack(s.coup_pad, 0, coup, sub)
        s.node_pad[...] = jnp.zeros((32, 4 * FD), F32)
        s.node_pad[3 * sub : 3 * sub + 6] = s.coup_pad[6:12]
        s.node_pad[16 + 3 * sub : 22 + 3 * sub] = s.coup_pad[0:6] * not_first
        high, low = halves(s.node_pad[...])
        s.node_rows[sub, 0:32] = high
        s.node_rows[sub, 32:64] = low

    def transposed(matrix, sub):
        width = matrix.shape[2]
        pad = s.coup_pad
        unpack(pad, 0, matrix, sub)
        value = pad[0:12, 0:width]
        high = value.astype(BF16).astype(F32)
        low = value - high
        pad[:, 0:width] = jnp.zeros((128, width), F32)
        pad[0:12, 0:width] = high
        pad[16:28, 0:width] = low
        pad[32:44, 0:width] = high
        pad[48:60, 0:width] = low
        return pad[:, 0:width].T.astype(BF16)

    for sub in range(2):
        s.coup_t[sub] = transposed(coup, sub)

    def make_block():
        own = s.blocks.at[app, z]
        for cycle in range(ny):
            value = s.line[app, cycle, 0:9]
            if cycle + 1 < ny:
                value = value + s.line[app, cycle + 1, 16:25]
            own[9 * cycle : 9 * cycle + 9] = value
        sums = s.line[app, 0, 9:13]
        for cycle in range(1, ny):
            sums = sums + s.line[app, cycle, 9:13]
        own[9 * ny : 9 * ny + 4] = sums

    for copy in number_copies:
        copy.wait_recv()
    s.number_z[z] = jnp.sum(s.number_y[...], axis=0)
    number_copies = to_all(s.number_z.at[z], s.z_sem, 0, z_peers)

    def rolled(index, value, start):
        s.twice[index, 0:FD] = value
        s.twice[index, FD : 2 * FD] = value
        return s.twice[index, pl.ds(start, FD)]

    ahead = lambda off: lax.rem(off + FD, FD)
    back = lambda off: lax.rem(FD - off, FD)
    on = lambda off: jnp.where(off >= 0, 1.0, 0.0).astype(F32)
    got_info_near.wait_recv()
    got_info_left.wait_recv()
    words = [
        pltpu.make_async_copy(s.info_near, s.word_near, s.word_sem.at[0]),
        pltpu.make_async_copy(s.info_left, s.word_left, s.word_sem.at[1]),
    ]
    for copy in words:
        copy.start()
    for copy in words:
        copy.wait()
    off_far = [offs[0, sub, 0] for sub in range(2)]
    off_right = [offs[0, sub, 1] for sub in range(2)]
    off_near = [s.word_near[sub, 0] for sub in range(2)]
    off_left = s.word_left[2, 0]
    on_far = [on(off) for off in off_far]
    on_right = [on(off) for off in off_right]
    on_near = [on(off) * not_first for off in off_near]
    on_left = on(off_left)

    def convert(turn):
        sub, part = chunks[turn]
        fetch(turn).wait()

        @pl.loop(0, FD // 64)
        def _(step):
            at_row = pl.multiple_of(step * 64, 64)
            high, low = halves(s.stage[turn, pl.ds(at_row, 64)])
            base = FD * (part % 2)
            s.flex_parts[sub, part // 2, pl.ds(base + at_row, 64)] = high
            s.flex_parts[sub, part // 2, pl.ds(2 * FD + base + at_row, 64)] = low

    for turn in range(8):
        convert(turn)

    for copy in number_copies:
        copy.wait_recv()
    s.number_x[x, k] = jnp.sum(s.number_z[...], axis=0)
    number_copies = to_all(s.number_x.at[x, k], s.x_sem, 0, x_peers)

    for sub in range(2):
        unpack(s.rows_pad, 12 * sub, rows, sub)
    high, low = halves(jnp.concatenate([s.rows_pad[...], jnp.zeros((8, rows.shape[2]), F32)], axis=0))
    s.rows_parts[0:32] = high
    s.rows_parts[32:64] = low
    s.y_own[...] = jnp.zeros(s.y_own.shape, F32)

    got_gap_near.wait_recv()
    got_gap_left.wait_recv()
    r0, w0, q0, w1, q1 = (s.vec.at[i] for i in range(5))
    for sub in range(2):
        r0[sub, face(FAR)] = gap[0, sub, 0] * on_far[sub]
        r0[sub, face(RIGHT)] = gap[0, sub, 1] * on_right[sub]
        r0[sub, face(NEAR)] = rolled(sub, s.gap_near[sub], ahead(off_near[sub])) * -on_near[sub]
    r0[0, face(LEFT)] = rolled(2, s.gap_left[...], ahead(off_left)) * -on_left
    r0[1, face(LEFT)] = rolled(3, gap[0, 0, 1], ahead(off_right[0])) * -on_right[0]

    owned = [(sub, part) for sub in range(2) for part in range(2)]

    def dot(first, second):
        total = None
        for sub, part in owned:
            term = jnp.sum(first(sub, part) * second(sub, part), axis=0, keepdims=True)
            total = term if total is None else total + term
        return total

    def of(vector):
        return lambda sub, part: vector[sub, face(2 * part + 1)]

    def product(sub, group):
        wide = jnp.dot(s.flex_parts[sub, group], s.split[sub], preferred_element_type=F32)
        s.moved[app, sub, 2 * FD * group : 2 * FD * (group + 1)] = quadrants(wide)

    def stacked(value):
        high, low = halves(value)
        return jnp.concatenate([high, high, low, low, jnp.zeros((64, RHS), BF16)], axis=0)

    def begin(vector, dots):
        for sub in range(2):
            high, low = halves(vector[sub])
            s.split[sub, :, 0:RHS] = high
            s.split[sub, :, RHS : 2 * RHS] = low
        wide = jnp.dot(s.node_rows[0], s.split[0], preferred_element_type=F32)
        wide = wide + jnp.dot(s.node_rows[1], s.split[1], preferred_element_type=F32)
        tile = s.line.at[app, y]
        tile[...] = quadrants(wide)
        tile[9:11] = jnp.concatenate(dots, axis=0)
        return to_all(tile, s.y_sem, app + 1, y_peers)

    def finish_faces(result, last):
        moved = s.total
        for sub in range(2):
            term = jnp.dot(s.coup_t[sub], stacked(s.y_own[app, sub]), preferred_element_type=F32)
            moved[sub] = s.moved[app, sub] + term

        def other(index, value, y_value):
            return value + jnp.dot(s.coup_t_n[index], stacked(y_value), preferred_element_type=F32)

        inner_left, inner_right = moved[1, face(LEFT)], moved[0, face(RIGHT)]
        result[0, face(RIGHT)] = (inner_right - rolled(0, inner_left, back(off_right[0]))) * on_right[0]
        if not last:
            result[1, face(LEFT)] = (inner_left - rolled(1, inner_right, ahead(off_right[0]))) * on_right[0]
        for copy in got_y:
            copy.wait_recv()
        for copy in got_faces:
            copy.wait_recv()
        for sub in range(2):
            value = other(sub, s.face_far[app, sub], s.y_far[app, sub]) * not_last
            jump = moved[sub, face(FAR)] - rolled(2 + sub, value, back(off_far[sub]))
            result[sub, face(FAR)] = jump * on_far[sub]
            if not last:
                value = other(2 + sub, s.face_near[app, sub], s.y_near[app, sub])
                jump = moved[sub, face(NEAR)] - rolled(4 + sub, value, ahead(off_near[sub]))
                result[sub, face(NEAR)] = jump * on_near[sub]
        value = other(5, s.face_right[app], s.y_right[app])
        jump = moved[1, face(RIGHT)] - rolled(6, value, back(off_right[1]))
        result[1, face(RIGHT)] = jump * on_right[1]
        if not last:
            value = other(4, s.face_left[app], s.y_left[app])
            jump = moved[0, face(LEFT)] - rolled(7, value, ahead(off_left))
            result[0, face(LEFT)] = jump * on_left

    def update(target, base, factor, step):
        for sub in range(2):
            for part in range(4):
                target[sub, face(part)] = base[sub, face(part)] + factor * step[sub, face(part)]

    got_picked = []

    def pick(first, stop):
        dofs = s.pick.shape[1]
        lane = lax.broadcasted_iota(jnp.int32, (8, 128), 1)
        for i in range(first, stop):
            xx, kk = x_line[i]
            tile = jnp.where(lane < 9 * ny, s.number_x[xx, kk], -1.0)
            column = jnp.concatenate([tile, jnp.zeros((120, 128), F32)], axis=0).T
            numbers = jnp.concatenate(
                [jnp.broadcast_to(column[0:BLOCK, j : j + 1], (BLOCK, 128)) for j in range(nz)], axis=0
            )
            for q in range(dofs // 128):
                wanted = (lax.broadcasted_iota(jnp.int32, numbers.shape, 1) + 128 * q).astype(F32)
                s.pick[:, 128 * q : 128 * q + 128] = jnp.where(numbers == wanted, 1.0, 0.0).astype(BF16)
            both = lax.dot_general(
                s.rows_parts[...],
                s.pick[...],
                (((1,), (1,)), ((), ())),
                preferred_element_type=F32,
            )
            own_rows = both[0:24] + both[32:56]
            if i == 0:
                s.picked_in[x, k] = own_rows
            else:
                s.picked[xx, kk] = own_rows
                got_picked.append(
                    send(s.picked.at[xx, kk], s.picked_in.at[x, k], s.pick_sem, (i - 1,), x_peers[i - 1])
                )

    none = jnp.zeros((1, RHS), F32)
    r1, p1, x2, r2, s1, w2 = (s.own.at[i] for i in range(6))
    plain = lambda vector: lambda sub, part: vector[sub, part]
    gamma, delta = [], []
    for app in range(APPS):
        last = app == APPS - 1
        if app == 0:
            vector, result, dots = r0, w0, [dot(of(r0), of(r0)), none]
        elif app == 1:
            vector, result, dots = w0, q0, [none, dot(of(r0), of(w0))]
        else:
            vector, result = w1, q1
            dots = [dot(plain(r1), plain(r1)), dot(plain(r1), of(w1))]
        got_line = begin(vector, dots)
        moved = s.moved.at[app]
        if app == 0:
            for copy in number_copies:
                copy.wait_recv()
            pick(0, nx)
        else:
            for sub in range(2):
                product(sub, 0)
        for copy in got_line:
            copy.wait_recv()
        make_block()
        got_z = to_all(s.blocks.at[app, z], s.z_sem, app + 1, z_peers)
        if app == 0:
            pick(nx, 2 * nx)
            for sub in range(2):
                product(sub, 0)
        got_faces = [send(moved.at[:, face(NEAR)], s.face_far.at[app], s.face_sem, (app, 0), (down, b))]
        if not last:
            got_faces.append(
                send(moved.at[:, face(FAR)], s.face_near.at[app], s.face_sem, (app, 1), (up, b))
            )
        for sub in range(2):
            product(sub, 1)
        got_faces.append(
            send(moved.at[0, face(LEFT)], s.face_right.at[app], s.face_sem, (app, 2), (y, left))
        )
        if not last:
            got_faces.append(
                send(moved.at[1, face(RIGHT)], s.face_left.at[app], s.face_sem, (app, 3), (y, right))
            )
        if app == 0:
            for copy in got_coup:
                copy.wait_recv()
            for sub in range(2):
                s.coup_t_n[sub] = transposed(s.coup_far, sub)
                s.coup_t_n[2 + sub] = transposed(s.coup_near, sub)
            s.coup_t_n[4] = transposed(s.coup_left, 1)
            s.coup_t_n[5] = transposed(s.coup_right, 0)
            for copy in got_picked:
                copy.wait_recv()
            for i in range(2 * nx):
                high, low = halves(s.picked_in[i // 2, i % 2])
                s.coarse[24 * i : 24 * i + 24] = high
                s.coarse[48 * nx + 24 * i : 48 * nx + 24 * i + 24] = low
        for copy in got_z:
            copy.wait_recv()
        loads = s.blocks[app]
        sums = jnp.sum(loads[:, BLOCK - 8 :, :], axis=0)
        high, low = halves(loads.reshape(nz * BLOCK, RHS))
        wide = jnp.dot(s.coarse[...], jnp.concatenate([high, low], axis=1), preferred_element_type=F32)
        parts = quadrants(wide)
        for i in range(2 * nx):
            s.part_out[app, i // 2, i % 2, 0:24] = parts[24 * i : 24 * i + 24]
            s.part_out[app, i // 2, i % 2, 24:32] = sums
        got_parts = []
        for i, (xx, kk) in enumerate(x_line):
            if i == 0:
                s.part_in[app, x, k] = s.part_out[app, x, k]
            else:
                got_parts.append(
                    send(
                        s.part_out.at[app, xx, kk],
                        s.part_in.at[app, x, k],
                        s.x_sem,
                        (app + 1, i - 1),
                        x_peers[i - 1],
                    )
                )
        for copy in got_parts:
            copy.wait_recv()
        ysum = s.part_in[app, 0, 0]
        for i in range(1, 2 * nx):
            ysum = ysum + s.part_in[app, i // 2, i % 2]
        sums = ysum[24:32]
        for sub in range(2):
            s.y_own[app, sub, 0:12] = ysum[12 * sub : 12 * sub + 12]
        y_own = s.y_own.at[app]
        got_y = [
            send(y_own, s.y_far.at[app], s.yv_sem, (app, 0), (down, b)),
            send(y_own.at[0], s.y_right.at[app], s.yv_sem, (app, 2), (y, left)),
        ]
        if not last:
            got_y += [
                send(y_own, s.y_near.at[app], s.yv_sem, (app, 1), (up, b)),
                send(y_own.at[1], s.y_left.at[app], s.yv_sem, (app, 3), (y, right)),
            ]
        finish_faces(result, last)
        first_row = 9 * ny - (BLOCK - 8)
        if app == 0:
            gamma.append(sums[first_row : first_row + 1])
        elif app == 1:
            delta.append(sums[first_row + 1 : first_row + 2])
            alpha0 = gamma[0] / delta[0]
            update(w1, w0, -alpha0, q0)
            for sub, part in owned:
                own = face(2 * part + 1)
                r1[sub, part] = r0[sub, own] - alpha0 * w0[sub, own]
        else:
            gamma.append(sums[first_row : first_row + 1])
            delta.append(sums[first_row + 1 : first_row + 2])

    beta1 = gamma[1] / gamma[0]
    alpha1 = gamma[1] / (delta[1] - beta1 * gamma[1] / alpha0)
    for sub, part in owned:
        own = face(2 * part + 1)
        z1 = q1[sub, own] + beta1 * q0[sub, own]
        s_value = w1[sub, own] + beta1 * w0[sub, own]
        p_value = r1[sub, part] + beta1 * r0[sub, own]
        s1[sub, part] = s_value
        p1[sub, part] = p_value
        x2[sub, part] = alpha0 * r0[sub, own] + alpha1 * p_value
        r2[sub, part] = r1[sub, part] - alpha1 * s_value
        w2[sub, part] = w1[sub, own] - alpha1 * z1

    sums = jnp.concatenate(
        [dot(plain(r2), plain(r2)), dot(plain(r2), plain(w2)), jnp.zeros((6, RHS), F32)], axis=0
    )
    base = 0
    for buffer, here, peers in (
        (s.end_y, (y,), y_peers),
        (s.end_z, (z,), z_peers),
        (s.end_x, (x, k), x_peers),
    ):
        buffer[here] = sums
        copies = [
            send(buffer.at[here], buffer.at[here], s.end_sem, (base + d,), peer)
            for d, peer in enumerate(peers)
        ]
        base += len(peers)
        for copy in copies:
            copy.wait_recv()
        sums = jnp.sum(buffer[...], axis=tuple(range(len(here))))
    gamma2, delta2 = sums[0:1], sums[1:2]
    beta2 = gamma2 / gamma[1]
    alpha2 = gamma2 / (delta2 - beta2 * gamma2 / alpha1)
    for sub, part in owned:
        mult_out[0, sub, part] = x2[sub, part] + alpha2 * (r2[sub, part] + beta2 * p1[sub, part])
        res_out[0, sub, part] = r2[sub, part] - alpha2 * (w2[sub, part] + beta2 * s1[sub, part])
    for copy in started:
        copy.wait_send()


def hand_on(mult_in, res_in, mult_out, res_out):
    mult_out[...] = mult_in[...]
    res_out[...] = res_in[...]


def per_device(ny, nx, nz, gap_load, offsets, corner_map, flexibility, coupling, corner_rows):
    shapes = scratch(ny, nx, nz, corner_rows.shape[-1])
    vmem, hbm = (pl.BlockSpec(memory_space=space) for space in (pltpu.VMEM, pltpu.HBM))
    out = jax.ShapeDtypeStruct(gap_load.shape, F32)

    results = pl.pallas_call(
        functools.partial(kernel, ny, nx, nz, tuple(shapes)),
        out_shape=(out, out),
        in_specs=[hbm] * 6,
        out_specs=(vmem, vmem),
        scratch_shapes=list(shapes.values()),
        compiler_params=pltpu.CompilerParams(
            collective_id=0, has_side_effects=True, vmem_limit_bytes=60 * 1024 * 1024
        ),
    )(gap_load, offsets, corner_map, coupling[0].transpose(1, 0, 2), corner_rows[0].transpose(1, 0, 2), flexibility)
    return pl.pallas_call(
        hand_on, out_shape=(out, out), in_specs=[vmem, vmem], out_specs=(vmem, vmem)
    )(*results)


def solution(mesh):
    ny, nb = mesh.shape["cuts"], mesh.shape["blk"]
    nz = 8 if nb == 64 else 2
    nx = nb // (2 * nz)
    in_specs = (
        P("cuts", "blk", None, None, None),
        P("cuts", "blk", None),
        P("cuts", "blk", None),
        P("cuts", "blk", None, None),
        P("cuts", "blk", None, None),
        P("cuts", "blk", None, None),
    )
    out_specs = (P("cuts", "blk", None, None, None), P("cuts", "blk", None, None, None))
    return jax.shard_map(
        functools.partial(per_device, ny, nx, nz),
        mesh=mesh,
        in_specs=in_specs,
        out_specs=out_specs,
        check_vma=False,
    )
```
